512 devices in a mesh: space: 128 (over z, y, core), fsdp: 4 (over x).
Axes of the slice: x: 4, y: 8, z: 8, core: 2. Of those that a mesh axis runs over, the one named last changes fastest.
Arguments:
- features: bfloat16 [65536, 256], P(('space', 'fsdp')), may hold values from -6 to 6
- cotangent: bfloat16 [65536, 128], P(('space', 'fsdp')), may hold values from -6 to 6
- weight: bfloat16 [256, 27, 128], P('fsdp'), may hold values from -0.078125 to 0.078125
- neighbour_map: int32 [27, 65536], P(None, ('space', 'fsdp')), may hold values from 0 to 416, as said below
- send_rows: int32 [16384], P(('space', 'fsdp')), may hold values from 0 to 128, as said below
Outputs:
- conv_out: bfloat16 [65536, 128], P(('space', 'fsdp'))
- grad_features: bfloat16 [65536, 256], P(('space', 'fsdp'))
- grad_weight: float32 [256, 27, 128], P('fsdp')
The draws below stay inside these ranges and needn't reach their ends.
Inputs may be any that keep to these rules, and one draw needn't show every extreme that they name: `send_rows`: each block's 32 entries name local rows 0 to 127 in its live slots, which come first, and 128 in the empty slots after them; a block has at least a third of 32 live slots, rounded up, and some block has all 32 live. `neighbour_map`: entry [k, v] is a row of the table of v's block: below 128 a local row, then the 32 slots of each of the 3 x 3 neighbouring lists, and 416 for no neighbour. Offset 27 // 2 names v's own row. No entry points at slots 128 + 4 * 32 to 287.
All inputs are finite; a program needn't handle non-finite values.
Results may differ from the reference program's by a relative error of at most 0.001.
Values may be sent and summed in bfloat16 or wider, within the bound.
A program may use at most 64 MiB of HBM per device.

```python
import math
import jax
import jax.numpy as jnp
from jax import lax

C_IN = 256
C_OUT = 128
KVOL = 27
V_DEV = 128
HC = 32
NV = 65536
SEND = 16384
N_SPACE = 128
N_FSDP = 4


def draw_send_rows(key, part):
    blocks = SEND // HC
    live_count = jax.random.randint(jax.random.fold_in(key, 11), (blocks,), (HC + 2) // 3, HC + 1)
    fullest = jax.random.randint(jax.random.fold_in(key, 12), (), 0, blocks)
    live_count = jnp.where(jnp.arange(blocks) == fullest, HC, live_count)
    row_picks = jax.random.randint(jax.random.fold_in(key, 13), (blocks, HC), 0, V_DEV)
    slot_index = jnp.arange(HC)[None, :]
    return jnp.where(slot_index < live_count[:, None], row_picks, V_DEV).reshape(SEND).astype(jnp.int32)


def draw_neighbour_map(key, part):
    category = jax.random.randint(jax.random.fold_in(key, 21), (KVOL, NV), 0, 10)
    local_rows = jax.random.randint(jax.random.fold_in(key, 22), (KVOL, NV), 0, V_DEV)
    which_list = jax.random.randint(jax.random.fold_in(key, 23), (KVOL, NV), 0, 8)
    which_list = which_list + (which_list >= 4).astype(jnp.int32)
    slot_pick = jax.random.randint(jax.random.fold_in(key, 24), (KVOL, NV), 0, HC)
    halo_rows = V_DEV + which_list * HC + slot_pick
    empty_row = V_DEV + 9 * HC
    picked = jnp.where(category < 6, local_rows, jnp.where(category < 9, halo_rows, empty_row))
    own_rows = jnp.arange(NV, dtype=jnp.int32) % V_DEV
    centre = jnp.arange(KVOL, dtype=jnp.int32)[:, None] == KVOL // 2
    return jnp.where(centre, own_rows[None, :], picked).astype(jnp.int32)


def steps_of(stream_key, dims, shards, least, top_value):
    def one(axis_at, blocks):
        heights = jax.random.uniform(jax.random.fold_in(jax.random.fold_in(stream_key, 6), axis_at), (blocks,), jnp.float32, least / len(shards), top_value / len(shards))
        return jnp.repeat(jnp.exp(heights), dims[axis_at] // blocks).reshape((-1,) + (1,) * (len(dims) - axis_at - 1))

    loudness = one(*shards[0])
    for cut in shards[1:]:
        loudness = loudness * one(*cut)
    return loudness


def gaussian(stream_key, extent, spread, reach, cuts=(), kind=jnp.bfloat16):
    drawn = jax.random.normal(stream_key, extent, jnp.float32) * spread
    if len(cuts) > 0:
        drawn = steps_of(stream_key, extent, cuts, -0.22, 0.18) * drawn
    return jnp.clip(drawn, min=-reach, max=reach).astype(kind)


def setup_inputs(seed: int = 0) -> dict:
    arg_keys = jax.random.split(jax.random.key(seed), 6)
    return {
        "features": gaussian(arg_keys[0], (NV, C_IN), 1.0, 6.0, ((0, 512),)),
        "cotangent": gaussian(arg_keys[1], (NV, C_OUT), 1.0, 6.0, ((0, 512),)),
        "weight": gaussian(arg_keys[2], (C_IN, KVOL, C_OUT), (KVOL * C_IN) ** -0.5, 0.078125, ((0, 4),)),
        "neighbour_map": draw_neighbour_map(jax.random.fold_in(arg_keys[5], 71), 0),
        "send_rows": draw_send_rows(jax.random.fold_in(arg_keys[5], 71), 0),
    }


def reference(features, cotangent, weight, neighbour_map, send_rows):
    blocks = N_SPACE * N_FSDP
    width_in = features.shape[1]
    width_out = cotangent.shape[1]
    table_len = V_DEV + 9 * HC + 1
    feature_blocks = features.reshape(blocks, V_DEV, width_in)
    grad_blocks = cotangent.reshape(blocks, V_DEV, width_out)
    map_blocks = jnp.transpose(neighbour_map.reshape(KVOL, blocks, V_DEV), (1, 0, 2))
    send_blocks = send_rows.reshape(blocks, HC)
    padded_feats = jnp.concatenate([feature_blocks, jnp.zeros((blocks, 1, width_in), features.dtype)], 1)

    def take_rows(block_rows, picks):
        return jnp.take(block_rows, picks, axis=0)
    boundary = jax.vmap(take_rows)(padded_feats, send_blocks)
    boundary = jnp.pad(boundary.reshape(N_SPACE, N_FSDP, HC, width_in), ((1, 1), (1, 1), (0, 0), (0, 0)))

    def block_step(carry, inputs):
        incoming, grad_weight = carry
        index, block_rows, block_grads, maps = inputs
        row_s = (index // N_FSDP).astype(jnp.int32)
        col_f = (index % N_FSDP).astype(jnp.int32)
        anchor = jnp.zeros((), jnp.int32)
        beside_all = lax.dynamic_slice(boundary, (row_s, col_f, anchor, anchor), (3, 3, HC, width_in))
        table = jnp.concatenate([block_rows, beside_all.reshape(9 * HC, width_in), jnp.zeros((1, width_in), block_rows.dtype)], 0)
        conv_acc = jnp.zeros((V_DEV, width_out), jnp.float32)
        table_grad = jnp.zeros((table_len, width_in), jnp.float32)
        weight_terms = []
        for offset in range(KVOL):
            picked = jnp.take(table, maps[offset], axis=0)
            kernel = weight[:, offset, :]
            conv_acc = conv_acc + jnp.dot(picked, kernel, preferred_element_type=jnp.float32)
            table_grad = table_grad.at[maps[offset]].add(jnp.dot(block_grads, kernel.T, preferred_element_type=jnp.float32))
            weight_terms.append(jnp.dot(picked.T, block_grads, preferred_element_type=jnp.float32))
        grad_weight = grad_weight + jnp.stack(weight_terms, 1)
        halo_part = table_grad[V_DEV:V_DEV + 9 * HC].reshape(3, 3, HC, width_in)
        window = lax.dynamic_slice(incoming, (row_s, col_f, anchor, anchor), (3, 3, HC, width_in))
        incoming = lax.dynamic_update_slice(incoming, window + halo_part, (row_s, col_f, anchor, anchor))
        return ((incoming, grad_weight), (conv_acc.astype(jnp.bfloat16), table_grad[:V_DEV]))
    start_state = (jnp.zeros((N_SPACE + 2, N_FSDP + 2, HC, width_in), jnp.float32), jnp.zeros((width_in, KVOL, width_out), jnp.float32))
    (incoming, grad_weight), (conv_blocks, local_grad) = lax.scan(block_step, start_state, (jnp.arange(blocks, dtype=jnp.int32), feature_blocks, grad_blocks, map_blocks))
    arriving = incoming[1:-1, 1:-1].reshape(blocks, HC, width_in)

    def settle(local_rows, picks, extra):
        padded = jnp.concatenate([local_rows, jnp.zeros((1, width_in), jnp.float32)], 0)
        return padded.at[picks].add(extra)[:V_DEV]
    grad_features = jax.vmap(settle)(local_grad, send_blocks, arriving)
    grad_scale = 1.0 / math.sqrt(NV)
    return (conv_blocks.reshape(NV, width_out), grad_features.reshape(NV, width_in).astype(jnp.bfloat16), grad_weight * grad_scale)
```

```python
import math

import jax
import jax.numpy as jnp
from jax import lax
from jax.experimental import pallas as pl
from jax.experimental.pallas import tpu as pltpu
from jax.sharding import PartitionSpec as P

MESH = pl.DeviceIdType.MESH
VMEM = pl.BlockSpec(memory_space=pltpu.VMEM)
SIDES = [(a, c) for a in range(3) for c in range(3) if (a, c) != (1, 1)]
NS, NF, NY, NZ = 128, 4, 8, 8
VOX, HC, CI, CO, KV, KP = 128, 32, 256, 128, 27, 28
IL = CI // NF
ROWS = KP * IL
HALF = ROWS // 2
PART = HALF // NY
TAB = VOX + 8 * HC
FSDP_ORDER = (2, 1, 3)


def position():
    s, f = lax.axis_index("space"), lax.axis_index("fsdp")
    core = lax.rem(s, 2)
    y = lax.rem(s // 2, NY)
    z = s // (2 * NY)
    return s, f, core, y, z


def shifted(s, f, ds, df):
    return (lax.rem(s + ds + NS, NS), lax.rem(f + df + NF, NF))


def meet(targets):
    barrier = pltpu.get_barrier_semaphore()
    for target in targets:
        pl.semaphore_signal(barrier, inc=1, device_id=target, device_id_type=MESH)
    pl.semaphore_wait(barrier, len(targets))


def remote(src, dst, send, recv, target):
    return pltpu.make_async_remote_copy(
        src_ref=src, dst_ref=dst, send_sem=send, recv_sem=recv, device_id=target, device_id_type=MESH
    )


def spread_kernel(b_ref, w_ref, beside_ref, wall_ref, hs, hr, xs, xr, ps, pr, own_sem):
    s, f, core, y, z = position()
    partner = (s + 1 - 2 * core, f)
    meet([shifted(s, f, 1 - a, 1 - c) for a, c in SIDES] + [shifted(s, f, 0, 2)] + [partner])
    copies = []
    for n, (a, c) in enumerate(SIDES):
        copies.append(remote(b_ref, beside_ref.at[n], hs.at[n], hr.at[n], shifted(s, f, 1 - a, 1 - c)))
        copies[-1].start()
    own = pltpu.make_async_copy(w_ref, wall_ref.at[f], own_sem)
    own.start()
    across = {}
    for d in FSDP_ORDER:
        target = shifted(s, f, 0, d)
        across[d] = remote(w_ref.at[core], wall_ref.at[f, core], xs.at[d], xr.at[d], target)
        across[d].start()
    handed = []
    for d in (1, 3, 2):
        source = lax.rem(f - d + NF, NF)
        got = wall_ref.at[source, core]
        remote(got, got, xs.at[d], xr.at[d], partner).wait_recv()
        handed.append((d, remote(got, got, ps.at[d], pr.at[d], partner)))
        handed[-1][1].start()
    for d, copy in handed:
        source = lax.rem(f - d + NF, NF)
        there = wall_ref.at[source, 1 - core]
        remote(there, there, ps.at[d], pr.at[d], partner).wait_recv()
        copy.wait_send()
    for d in FSDP_ORDER:
        across[d].wait_send()
    own.wait()
    for copy in copies:
        copy.wait()


def compute_kernel(feat_ref, beside_ref, map_ref, mapt_ref, cot_ref, w_ref, conv_ref, gw_ref, own_ref, halo_ref, tab, tg):
    tab[:VOX, :] = feat_ref[...]
    tab[VOX:, :] = beside_ref[...].reshape(8 * HC, CI)
    cot = cot_ref[...]
    lanes = lax.broadcasted_iota(jnp.int32, (VOX, TAB), 1)
    rows = lax.broadcasted_iota(jnp.int32, (TAB, VOX), 0)
    acc = jnp.zeros((VOX, CO), jnp.float32)
    scale = 1.0 / math.sqrt(NS * NF * VOX)
    group = 3
    for g in range(KV // group):
        hot, high, low = [], [], []
        for k in range(g * group, (g + 1) * group):
            col = mapt_ref[:, k : k + 1]
            pick = (lanes == col).astype(jnp.bfloat16)
            picked = jnp.dot(pick, tab[...], preferred_element_type=jnp.float32).astype(jnp.bfloat16)
            kernel = w_ref[:, k].reshape(CI, CO)
            acc = acc + jnp.dot(picked, kernel, preferred_element_type=jnp.float32)
            gw = lax.dot_general(picked, cot, (((0,), (0,)), ((), ())), preferred_element_type=jnp.float32) * scale
            for q in range(NF):
                gw_ref[q, k * IL : (k + 1) * IL, :] = gw[q * IL : (q + 1) * IL]
            term = lax.dot_general(cot, kernel, (((1,), (1,)), ((), ())), preferred_element_type=jnp.float32)
            top = term.astype(jnp.bfloat16)
            high.append(top)
            low.append((term - top.astype(jnp.float32)).astype(jnp.bfloat16))
            hot.append((rows == map_ref[k : k + 1, :]).astype(jnp.bfloat16))
        hot_all = jnp.concatenate(hot, 1)
        both = jnp.concatenate([jnp.concatenate(high, 0), jnp.concatenate(low, 0)], 1)
        new = jnp.dot(hot_all, both, preferred_element_type=jnp.float32)
        if g == 0:
            tg[...] = new
        else:
            tg[...] += new
    gw_ref[:, KV * IL :, :] = jnp.zeros((NF, IL, CO), jnp.float32)
    conv_ref[...] = acc.astype(jnp.bfloat16)
    own_ref[...] = tg[:VOX, :CI] + tg[:VOX, CI:]
    halo_ref[...] = (tg[VOX:, :CI] + tg[VOX:, CI:]).reshape(8, HC, CI)


def reduce_kernel(gw_ref, halo_ref, total_ref, back_ref, pbuf, acc0, xbuf, acc1, ybuf, acc2, zbuf,
                  hs, hr, ps, pr, xs, xr, ys, yr, zs, zr, gs, gr, cs, cr):
    s, f, core, y, z = position()
    other = 1 - core
    partner = (s + 1 - 2 * core, f)

    def y_peer(d):
        return ((z * NY + lax.rem(y + d, NY)) * 2 + core, f)

    def z_peer(d):
        return ((lax.rem(z + d, NZ) * NY + y) * 2 + core, f)

    meet(
        [shifted(s, f, a - 1, c - 1) for a, c in SIDES]
        + [partner]
        + [shifted(s, f, 0, 2)]
        + [y_peer(d) for d in range(1, NY)]
        + [z_peer(d) for d in range(1, NZ)]
    )
    order = (2, 1, 3, 0)
    pairs = {}
    for d in order:
        j = lax.rem(f + d, NF)
        src = gw_ref.at[j, pl.ds(other * HALF, HALF), :]
        pairs[d] = remote(src, pbuf.at[d], ps.at[d], pr.at[d], partner)
        pairs[d].start()
    copies = []
    for n, (a, c) in enumerate(SIDES):
        copies.append(remote(halo_ref.at[n], back_ref.at[n], hs.at[n], hr.at[n], shifted(s, f, a - 1, c - 1)))
        copies[-1].start()
    across = {}
    for d in order:
        j = lax.rem(f + d, NF)
        pairs[d].wait_recv()

        def add_pair(i, _):
            here = pl.ds(pl.multiple_of(i * PART, 8), PART)
            mine = pl.ds(pl.multiple_of(core * HALF + i * PART, 8), PART)
            acc0[d, here, :] = gw_ref[j, mine, :] + pbuf[d, here, :]
            return 0

        lax.fori_loop(0, NY, add_pair, 0)
        if d != 0:
            across[d] = remote(acc0.at[d], xbuf.at[d - 1], xs.at[d], xr.at[d], shifted(s, f, 0, d))
            across[d].start()
    for d in FSDP_ORDER:
        across[d].wait_recv()

    def add_x(i, _):
        here = pl.ds(pl.multiple_of(i * PART, 8), PART)
        acc1[i] = (acc0[0, here, :] + xbuf[0, here, :]) + (xbuf[1, here, :] + xbuf[2, here, :])
        return 0

    lax.fori_loop(0, NY, add_x, 0)
    y_copies = []
    for d in range(1, NY):
        y_copies.append(remote(acc1.at[lax.rem(y + d, NY)], ybuf.at[d], ys.at[d], yr.at[d], y_peer(d)))
        y_copies[-1].start()
    for copy in y_copies:
        copy.wait_recv()
    running = acc1[y]
    for d in range(1, NY):
        running = running + ybuf[d]
    acc2[...] = running
    zbuf[z] = running
    z_copies = []
    for d in range(1, NZ):
        z_copies.append(remote(acc2, zbuf.at[z], zs.at[d], zr.at[d], z_peer(d)))
        z_copies[-1].start()
    for d in range(1, NZ):
        from_z = zbuf.at[lax.rem(z - d + NZ, NZ)]
        remote(from_z, from_z, zs.at[d], zr.at[d], partner).wait_recv()
    done = zbuf[0]
    for q in range(1, NZ):
        done = done + zbuf[q]

    def spot(side, at):
        return total_ref.at[side * NY + at]

    total_ref[core * NY + y] = done
    mine = spot(core, y)
    g_copies = []
    for d in range(1, NY):
        g_copies.append(remote(mine, mine, gs.at[d], gr.at[d], y_peer(d)))
        g_copies[-1].start()
    handed = [remote(mine, mine, cs.at[0], cr.at[0], partner)]
    handed[0].start()
    for d in range(1, NY):
        got = spot(core, lax.rem(y - d + NY, NY))
        remote(got, got, gs.at[d], gr.at[d], partner).wait_recv()
        handed.append(remote(got, got, cs.at[d], cr.at[d], partner))
        handed[-1].start()
    for d in range(NY):
        there = spot(other, lax.rem(y - d + NY, NY))
        remote(there, there, cs.at[d], cr.at[d], partner).wait_recv()
        handed[d].wait_send()
    for copy in copies:
        copy.wait()
    for d in order:
        pairs[d].wait_send()
    for d in FSDP_ORDER:
        across[d].wait_send()
    for copy in y_copies + z_copies + g_copies:
        copy.wait_send()


def dma(n):
    return pltpu.SemaphoreType.DMA((n,))


def body(features, cotangent, weight, neighbour_map, send_rows):
    f32, bf16 = jnp.float32, jnp.bfloat16
    pick = (send_rows[:, None] == jnp.arange(VOX)[None, :]).astype(bf16)
    boundary = jnp.dot(pick, features, preferred_element_type=f32).astype(bf16)
    by_offset = jnp.pad(jnp.transpose(weight, (1, 0, 2)), ((0, 1), (0, 0), (0, 0)))
    beside, wall = pl.pallas_call(
        spread_kernel,
        out_shape=(
            jax.ShapeDtypeStruct((8, HC, CI), bf16),
            jax.ShapeDtypeStruct((NF, 2, KP // 2, IL, CO), bf16),
        ),
        in_specs=[VMEM] * 2,
        out_specs=(VMEM, VMEM),
        scratch_shapes=[dma(8), dma(8), dma(NF), dma(NF), dma(NF), dma(NF), pltpu.SemaphoreType.DMA],
        compiler_params=pltpu.CompilerParams(collective_id=0, has_side_effects=True),
        name="spread",
    )(boundary, by_offset.reshape(2, KP // 2, IL, CO))
    s, f = lax.axis_index("space"), lax.axis_index("fsdp")

    def inside(sign):
        ok = [
            (s + sign * (a - 1) >= 0) & (s + sign * (a - 1) < NS) & (f + sign * (c - 1) >= 0) & (f + sign * (c - 1) < NF)
            for a, c in SIDES
        ]
        return jnp.stack(ok)[:, None, None]

    beside = jnp.where(inside(1), beside, jnp.zeros_like(beside))
    spots = jnp.where(neighbour_map >= VOX + 5 * HC, neighbour_map - HC, neighbour_map)
    conv_out, gw, own, halo = pl.pallas_call(
        compute_kernel,
        out_shape=(
            jax.ShapeDtypeStruct((VOX, CO), bf16),
            jax.ShapeDtypeStruct((NF, ROWS, CO), f32),
            jax.ShapeDtypeStruct((VOX, CI), f32),
            jax.ShapeDtypeStruct((8, HC, CI), f32),
        ),
        in_specs=[VMEM] * 6,
        out_specs=(VMEM,) * 4,
        scratch_shapes=[pltpu.VMEM((TAB, CI), bf16), pltpu.VMEM((TAB, 2 * CI), f32)],
        compiler_params=pltpu.CompilerParams(vmem_limit_bytes=40 << 20),
        name="stencil",
    )(features, beside, spots, spots.T, cotangent, wall.reshape(NF, KP, IL, CO))
    total, back = pl.pallas_call(
        reduce_kernel,
        out_shape=(
            jax.ShapeDtypeStruct((2 * NY, PART, CO), f32),
            jax.ShapeDtypeStruct((8, HC, CI), f32),
        ),
        in_specs=[VMEM] * 2,
        out_specs=(VMEM, VMEM),
        scratch_shapes=[
            pltpu.VMEM((NF, HALF, CO), f32),
            pltpu.VMEM((NF, HALF, CO), f32),
            pltpu.VMEM((NF - 1, HALF, CO), f32),
            pltpu.VMEM((NY, PART, CO), f32),
            pltpu.VMEM((NY, PART, CO), f32),
            pltpu.VMEM((PART, CO), f32),
            pltpu.VMEM((NZ, PART, CO), f32),
        ]
        + [dma(8)] * 2 + [dma(NF)] * 4 + [dma(NY)] * 2 + [dma(NZ)] * 2 + [dma(NY)] * 4,
        compiler_params=pltpu.CompilerParams(collective_id=1, has_side_effects=True, vmem_limit_bytes=40 << 20),
        name="reduce",
    )(gw, halo)
    incoming = jnp.sum(jnp.where(inside(-1), back, 0.0), 0)
    put = (jnp.arange(VOX)[:, None] == send_rows[None, :]).astype(f32)
    settled = own + jnp.dot(put, incoming, preferred_element_type=f32, precision=lax.Precision.HIGHEST)
    grad_weight = jnp.transpose(total.reshape(KP, IL, CO)[:KV], (1, 0, 2))
    return (conv_out, settled.astype(bf16), grad_weight)


def solution(mesh):
    rows = P(("space", "fsdp"), None)
    placed = (rows, rows, P("fsdp", None, None), P(None, ("space", "fsdp")), P(("space", "fsdp")))
    return jax.shard_map(
        body, mesh=mesh, in_specs=placed, out_specs=(rows, rows, P("fsdp", None, None)), check_vma=False
    )
```

```python
import math

import jax
import jax.numpy as jnp
from jax import lax
from jax.experimental import pallas as pl
from jax.experimental.pallas import tpu as pltpu
from jax.sharding import PartitionSpec as P

MESH = pl.DeviceIdType.MESH
VMEM = pl.BlockSpec(memory_space=pltpu.VMEM)
SIDES = [(a, c) for a in range(3) for c in range(3) if (a, c) != (1, 1)]
NS, NF, NY, NZ = 128, 4, 8, 8
VOX, HC, CI, CO, KV, KP = 128, 32, 256, 128, 27, 28
IL = CI // NF
ROWS = KP * IL
HALF = ROWS // 2
LINE = HALF // 2
SKIP = KV // 2
CHUNK = LINE // NY
PART = 112
TAB = VOX + 8 * HC


def position():
    s, f = lax.axis_index("space"), lax.axis_index("fsdp")
    core = lax.rem(s, 2)
    y = lax.rem(s // 2, NY)
    z = s // (2 * NY)
    return s, f, core, y, z


def shifted(s, f, ds, df):
    return (lax.rem(s + ds + NS, NS), lax.rem(f + df + NF, NF))


def meet(targets):
    barrier = pltpu.get_barrier_semaphore()
    for target in targets:
        pl.semaphore_signal(barrier, inc=1, device_id=target, device_id_type=MESH)
    pl.semaphore_wait(barrier, len(targets))


def remote(src, dst, send, recv, target):
    return pltpu.make_async_remote_copy(
        src_ref=src, dst_ref=dst, send_sem=send, recv_sem=recv, device_id=target, device_id_type=MESH
    )


def spread_kernel(b_ref, w_ref, beside_ref, wall_ref, hs, hr, xs, xr, ps, pr, own_sem):
    s, f, core, y, z = position()
    partner = (s + 1 - 2 * core, f)
    left, right = shifted(s, f, 0, -1), shifted(s, f, 0, 1)
    from_left, from_right, opposite = left[1], right[1], lax.rem(f + 2, NF)
    meet([shifted(s, f, 1 - a, 1 - c) for a, c in SIDES] + [partner])
    copies = []
    for n, (a, c) in enumerate(SIDES):
        copies.append(remote(b_ref, beside_ref.at[n], hs.at[n], hr.at[n], shifted(s, f, 1 - a, 1 - c)))
        copies[-1].start()
    own = [pltpu.make_async_copy(w_ref.at[pl.ds(h * SKIP, SKIP + 1)], wall_ref.at[f, h], own_sem.at[h]) for h in range(2)]
    own[0].start()
    own[1].start()
    quarter = KP // 4
    first, second = pl.ds(0, quarter), pl.ds(quarter, quarter)
    mine = w_ref.at[pl.ds(core * SKIP, SKIP + 1)]
    across = [
        remote(mine, wall_ref.at[f, core], xs.at[0], xr.at[0], right),
        remote(mine, wall_ref.at[f, core], xs.at[1], xr.at[1], left),
    ]
    across[0].start()
    across[1].start()

    def landed(side):
        return (
            wall_ref.at[from_left, side],
            wall_ref.at[from_right, side],
            wall_ref.at[opposite, side, first],
            wall_ref.at[opposite, side, second],
        )

    handed = []
    for m, got in enumerate(landed(core)):
        remote(got, got, xs.at[m], xr.at[m], partner).wait_recv()
        if m == 0:
            piece = wall_ref.at[from_left, core, first]
            across.append(remote(piece, piece, xs.at[2], xr.at[2], right))
            across[-1].start()
        if m == 1:
            piece = wall_ref.at[from_right, core, second]
            across.append(remote(piece, piece, xs.at[3], xr.at[3], left))
            across[-1].start()
        handed.append(remote(got, got, ps.at[m], pr.at[m], partner))
        handed[-1].start()
    for m, there in enumerate(landed(1 - core)):
        remote(there, there, ps.at[m], pr.at[m], partner).wait_recv()
    for copy in handed + across:
        copy.wait_send()
    own[0].wait()
    own[1].wait()
    for copy in copies:
        copy.wait()


def compute_kernel(feat_ref, beside_ref, map_ref, mapt_ref, cot_ref, w_ref, conv_ref, gw_ref, own_ref, halo_ref, tab, tg):
    tab[:VOX, :] = feat_ref[...]
    s, f, core, y, z = position()
    for n, (a, c) in enumerate(SIDES):
        outer, inner = s + a - 1, f + c - 1
        ok = (outer >= 0) & (outer < NS) & (inner >= 0) & (inner < NF)
        rows_n = beside_ref[n]
        tab[VOX + n * HC : VOX + (n + 1) * HC, :] = jnp.where(ok, rows_n, jnp.zeros_like(rows_n))
    cot = cot_ref[...]
    lanes = lax.broadcasted_iota(jnp.int32, (VOX, TAB), 1)
    rows = lax.broadcasted_iota(jnp.int32, (TAB, VOX), 0)
    acc = jnp.zeros((VOX, CO), jnp.float32)
    scale = 1.0 / math.sqrt(NS * NF * VOX)
    group = 3
    for g in range(KV // group):
        hot, high, low = [], [], []
        for k in range(g * group, (g + 1) * group):
            col = mapt_ref[:, k : k + 1]
            pick = (lanes == col).astype(jnp.bfloat16)
            picked = jnp.dot(pick, tab[...], preferred_element_type=jnp.float32).astype(jnp.bfloat16)
            kernel = w_ref[:, k // (SKIP + 1), k - k // (SKIP + 1) * SKIP].reshape(CI, CO)
            acc = acc + jnp.dot(picked, kernel, preferred_element_type=jnp.float32)
            gw = lax.dot_general(picked, cot, (((0,), (0,)), ((), ())), preferred_element_type=jnp.float32) * scale
            for q in range(NF):
                gw_ref[q, k * IL : (k + 1) * IL, :] = gw[q * IL : (q + 1) * IL]
            term = lax.dot_general(cot, kernel, (((1,), (1,)), ((), ())), preferred_element_type=jnp.float32)
            top = term.astype(jnp.bfloat16)
            high.append(top)
            low.append((term - top.astype(jnp.float32)).astype(jnp.bfloat16))
            hot.append((rows == map_ref[k : k + 1, :]).astype(jnp.bfloat16))
        hot_all = jnp.concatenate(hot, 1)
        both = jnp.concatenate([jnp.concatenate(high, 0), jnp.concatenate(low, 0)], 1)
        new = jnp.dot(hot_all, both, preferred_element_type=jnp.float32)
        if g == 0:
            tg[...] = new
        else:
            tg[...] += new
    gw_ref[:, KV * IL :, :] = jnp.zeros((NF, IL, CO), jnp.float32)
    conv_ref[...] = acc.astype(jnp.bfloat16)
    own_ref[...] = tg[:VOX, :CI] + tg[:VOX, CI:]
    halo_ref[...] = (tg[VOX:, :CI] + tg[VOX:, CI:]).reshape(8, HC, CI)


def reduce_kernel(gw_ref, halo_ref, total_ref, back_ref, pbuf, acc0, rbuf, xbuf, acc1, ubuf, acc2, vbuf,
                  hs, hr, ps, pr, xs, xr, us, ur, vs, vr, gs, gr, cs, cr):
    s, f, core, y, z = position()
    other = 1 - core
    partner = (s + 1 - 2 * core, f)
    left, right = shifted(s, f, 0, -1), shifted(s, f, 0, 1)

    def y_peer(d):
        return ((z * NY + lax.rem(y + d, NY)) * 2 + core, f)

    def z_peer(d):
        return ((lax.rem(z + d, NZ) * NY + y) * 2 + core, f)

    lines = ((y, y_peer), (z, z_peer))
    meet(
        [shifted(s, f, a - 1, c - 1) for a, c in SIDES]
        + [partner]
        + [y_peer(d) for d in range(1, NY)]
        + [z_peer(d) for d in range(1, NZ)]
    )
    order = (2, 1, 3, 0)
    pairs = {}
    for d in order:
        src = gw_ref.at[lax.rem(f + d, NF), pl.ds(other * HALF, HALF), :]
        pairs[d] = remote(src, pbuf.at[d], ps.at[d], pr.at[d], partner)
        pairs[d].start()
    copies = []
    for n, (a, c) in enumerate(SIDES):
        copies.append(remote(halo_ref.at[n], back_ref.at[n], hs.at[n], hr.at[n], shifted(s, f, a - 1, c - 1)))
        copies[-1].start()
    half_a, half_b = pl.ds(0, LINE), pl.ds(LINE, LINE)
    across = {}

    def send_x(m, src, dst, target):
        across[m] = remote(src, dst, xs.at[m], xr.at[m], target)
        across[m].start()

    for d in order:
        j = lax.rem(f + d, NF)
        pairs[d].wait_recv()

        def add_pair(i, _):
            here = pl.ds(pl.multiple_of(i * PART, 8), PART)
            mine = pl.ds(pl.multiple_of(core * HALF + i * PART, 8), PART)
            acc0[d, here, :] = gw_ref[j, mine, :] + pbuf[d, here, :]
            return 0

        lax.fori_loop(0, HALF // PART, add_pair, 0)
        if d == 2:
            send_x(0, acc0.at[2, half_a], rbuf.at[0], right)
            send_x(1, acc0.at[2, half_b], rbuf.at[1], left)
        if d == 1:
            send_x(2, acc0.at[1, half_b], xbuf.at[0, half_b], right)
        if d == 3:
            send_x(3, acc0.at[3, half_a], xbuf.at[1, half_a], left)

    for m, d, begin, half, target in ((0, 1, 0, half_a, right), (1, 3, LINE, half_b, left)):
        across[m].wait_recv()

        def add_relay(i, _):
            here = pl.ds(pl.multiple_of(begin + i * PART, 8), PART)
            acc0[d, here, :] += rbuf[m, pl.ds(pl.multiple_of(i * PART, 8), PART), :]
            return 0

        lax.fori_loop(0, LINE // PART, add_relay, 0)
        send_x(4 + m, acc0.at[d, half], xbuf.at[m, half], target)

    u_copies = []
    for t, needs in enumerate(((3, 4), (2, 5))):
        for m in needs:
            across[m].wait_recv()

        def add_x(i, _):
            here = pl.ds(pl.multiple_of(t * LINE + i * CHUNK, 8), CHUNK)
            acc1[t, i] = acc0[0, here, :] + (xbuf[0, here, :] + xbuf[1, here, :])
            return 0

        lax.fori_loop(0, NY, add_x, 0)
        at, peer = lines[t]
        for d in range(1, NY):
            u_copies.append(remote(acc1.at[t, lax.rem(at + d, NY)], ubuf.at[t, d], us.at[t, d], ur.at[t, d], peer(d)))
            u_copies[-1].start()
    v_copies = []
    for t in range(2):
        for copy in u_copies[t * 7 : t * 7 + 7]:
            copy.wait_recv()
        running = acc1[t, lines[t][0]]
        for d in range(1, NY):
            running = running + ubuf[t, d]
        acc2[t] = running
        at, peer = lines[1 - t]
        vbuf[t, at] = running
        for d in range(1, NZ):
            v_copies.append(remote(acc2.at[t], vbuf.at[t, at], vs.at[t, d], vr.at[t, d], peer(d)))
            v_copies[-1].start()
    g_copies, handed = [], []
    for t in range(2):
        across_at = lines[1 - t][0]
        for d in range(1, NZ):
            got = vbuf.at[t, lax.rem(across_at - d + NZ, NZ)]
            remote(got, got, vs.at[t, d], vr.at[t, d], partner).wait_recv()
        done = vbuf[t, 0]
        for q in range(1, NZ):
            done = done + vbuf[t, q]
        at, peer = lines[t]
        total_ref[core, t, at] = done
        mine = total_ref.at[core, t, at]
        for d in range(1, NY):
            g_copies.append(remote(mine, mine, gs.at[t, d], gr.at[t, d], peer(d)))
            g_copies[-1].start()
        handed.append(remote(mine, mine, cs.at[t, 0], cr.at[t, 0], partner))
        handed[-1].start()
    for copy in copies:
        copy.wait()
    for d in range(1, NY):
        for t in range(2):
            got = total_ref.at[core, t, lax.rem(lines[t][0] - d + NY, NY)]
            remote(got, got, gs.at[t, d], gr.at[t, d], partner).wait_recv()
            handed.append(remote(got, got, cs.at[t, d], cr.at[t, d], partner))
            handed[-1].start()
    for d in range(NY):
        for t in range(2):
            there = total_ref.at[other, t, lax.rem(lines[t][0] - d + NY, NY)]
            remote(there, there, cs.at[t, d], cr.at[t, d], partner).wait_recv()
    for copy in handed + u_copies + v_copies + g_copies:
        copy.wait_send()
    for d in order:
        pairs[d].wait_send()
    for m in range(6):
        across[m].wait_send()


def dma(n):
    return pltpu.SemaphoreType.DMA((n,))


def body(features, cotangent, weight, neighbour_map, send_rows):
    f32, bf16 = jnp.float32, jnp.bfloat16
    pick = (send_rows[:, None] == jnp.arange(VOX)[None, :]).astype(bf16)
    boundary = jnp.dot(pick, features, preferred_element_type=f32).astype(bf16)
    by_offset = jnp.transpose(weight, (1, 0, 2))
    beside, wall = pl.pallas_call(
        spread_kernel,
        out_shape=(
            jax.ShapeDtypeStruct((8, HC, CI), bf16),
            jax.ShapeDtypeStruct((NF, 2, KP // 2, IL, CO), bf16),
        ),
        in_specs=[VMEM] * 2,
        out_specs=(VMEM, VMEM),
        scratch_shapes=[dma(8), dma(8), dma(4), dma(4), dma(4), dma(4), dma(2)],
        compiler_params=pltpu.CompilerParams(collective_id=0, has_side_effects=True),
        name="spread",
    )(boundary, by_offset)
    s, f = lax.axis_index("space"), lax.axis_index("fsdp")

    def inside(sign):
        ok = [
            (s + sign * (a - 1) >= 0) & (s + sign * (a - 1) < NS) & (f + sign * (c - 1) >= 0) & (f + sign * (c - 1) < NF)
            for a, c in SIDES
        ]
        return jnp.stack(ok)[:, None, None]

    spots = jnp.where(neighbour_map >= VOX + 5 * HC, neighbour_map - HC, neighbour_map)
    conv_out, gw, own, halo = pl.pallas_call(
        compute_kernel,
        out_shape=(
            jax.ShapeDtypeStruct((VOX, CO), bf16),
            jax.ShapeDtypeStruct((NF, ROWS, CO), f32),
            jax.ShapeDtypeStruct((VOX, CI), f32),
            jax.ShapeDtypeStruct((8, HC, CI), f32),
        ),
        in_specs=[VMEM] * 6,
        out_specs=(VMEM,) * 4,
        scratch_shapes=[pltpu.VMEM((TAB, CI), bf16), pltpu.VMEM((TAB, 2 * CI), f32)],
        compiler_params=pltpu.CompilerParams(vmem_limit_bytes=40 << 20),
        name="stencil",
    )(features, beside, spots, spots.T, cotangent, wall)
    total, back = pl.pallas_call(
        reduce_kernel,
        out_shape=(
            jax.ShapeDtypeStruct((2, 2, NY, CHUNK, CO), f32),
            jax.ShapeDtypeStruct((8, HC, CI), f32),
        ),
        in_specs=[VMEM] * 2,
        out_specs=(VMEM, VMEM),
        scratch_shapes=[
            pltpu.VMEM((NF, HALF, CO), f32),
            pltpu.VMEM((NF, HALF, CO), f32),
            pltpu.VMEM((2, LINE, CO), f32),
            pltpu.VMEM((2, HALF, CO), f32),
            pltpu.VMEM((2, NY, CHUNK, CO), f32),
            pltpu.VMEM((2, NY, CHUNK, CO), f32),
            pltpu.VMEM((2, CHUNK, CO), f32),
            pltpu.VMEM((2, NZ, CHUNK, CO), f32),
        ]
        + [dma(8)] * 2 + [dma(NF)] * 2 + [dma(6)] * 2 + [pltpu.SemaphoreType.DMA((2, NY))] * 8,
        compiler_params=pltpu.CompilerParams(collective_id=1, has_side_effects=True, vmem_limit_bytes=40 << 20),
        name="reduce",
    )(gw, halo)
    incoming = jnp.sum(jnp.where(inside(-1), back, 0.0), 0)
    put = (jnp.arange(VOX)[:, None] == send_rows[None, :]).astype(f32)
    settled = own + jnp.dot(put, incoming, preferred_element_type=f32, precision=lax.Precision.HIGHEST)
    grad_weight = jnp.transpose(total.reshape(KP, IL, CO)[:KV], (1, 0, 2))
    return (conv_out, settled.astype(bf16), grad_weight)


def solution(mesh):
    rows = P(("space", "fsdp"), None)
    placed = (rows, rows, P("fsdp", None, None), P(None, ("space", "fsdp")), P(("space", "fsdp")))
    return jax.shard_map(
        body, mesh=mesh, in_specs=placed, out_specs=(rows, rows, P("fsdp", None, None)), check_vma=False
    )
```

```python
import math

import jax
import jax.numpy as jnp
from jax import lax
from jax.experimental import pallas as pl
from jax.experimental.pallas import tpu as pltpu
from jax.sharding import PartitionSpec as P

MESH = pl.DeviceIdType.MESH
VMEM = pl.BlockSpec(memory_space=pltpu.VMEM)
SIDES = [(a, c) for a in range(3) for c in range(3) if (a, c) != (1, 1)]
NS, NF, NY, NZ = 128, 4, 8, 8
VOX, HC, CI, CO, KV, KP = 128, 32, 256, 128, 27, 28
IL = CI // NF
ROWS = KP * IL
HALF = ROWS // 2
LINE = HALF // 2
SKIP = KV // 2
CHUNK = LINE // NY
PART = 112
TAB = VOX + 8 * HC


def position():
    s, f = lax.axis_index("space"), lax.axis_index("fsdp")
    core = lax.rem(s, 2)
    y = lax.rem(s // 2, NY)
    z = s // (2 * NY)
    return s, f, core, y, z


def shifted(s, f, ds, df):
    return (lax.rem(s + ds + NS, NS), lax.rem(f + df + NF, NF))


def meet(targets):
    barrier = pltpu.get_barrier_semaphore()
    for target in targets:
        pl.semaphore_signal(barrier, inc=1, device_id=target, device_id_type=MESH)
    pl.semaphore_wait(barrier, len(targets))


def remote(src, dst, send, recv, target):
    return pltpu.make_async_remote_copy(
        src_ref=src, dst_ref=dst, send_sem=send, recv_sem=recv, device_id=target, device_id_type=MESH
    )


def whole_kernel(b_ref, w_ref, feat_ref, map_ref, cot_ref, conv_ref, own_ref, total_ref, back_ref,
                 beside_ref, wall_ref, tab, tab_t, seen, gw_ref, tg, halo_ref, pbuf, acc0, rbuf, xbuf, acc1, ubuf, acc2, vbuf,
                 bs, br, ws, wr, hands, handr, own_sem,
                 hs, hr, ps, pr, xs, xr, us, ur, vs, vr, gs, gr, cs, cr):
    s, f, core, y, z = position()
    other = 1 - core
    partner = (s + 1 - 2 * core, f)
    left, right = shifted(s, f, 0, -1), shifted(s, f, 0, 1)
    from_left, from_right, opposite = left[1], right[1], lax.rem(f + 2, NF)

    def y_peer(d):
        return ((z * NY + lax.rem(y + d, NY)) * 2 + core, f)

    def z_peer(d):
        return ((lax.rem(z + d, NZ) * NY + y) * 2 + core, f)

    lines = ((y, y_peer), (z, z_peer))
    meet(
        [shifted(s, f, a - 1, c - 1) for a, c in SIDES]
        + [partner]
        + [y_peer(d) for d in range(1, NY)]
        + [z_peer(d) for d in range(1, NZ)]
    )
    spread = []
    for n, (a, c) in enumerate(SIDES):
        spread.append(remote(b_ref, beside_ref.at[n], bs.at[n], br.at[n], shifted(s, f, 1 - a, 1 - c)))
        spread[-1].start()
    own = [pltpu.make_async_copy(w_ref.at[pl.ds(h * SKIP, SKIP + 1)], wall_ref.at[f, h], own_sem.at[h]) for h in range(2)]
    own[0].start()
    own[1].start()
    quarter = KP // 4
    first, second = pl.ds(0, quarter), pl.ds(quarter, quarter)
    half_w = w_ref.at[pl.ds(core * SKIP, SKIP + 1)]
    wide = [
        remote(half_w, wall_ref.at[f, core], ws.at[0], wr.at[0], right),
        remote(half_w, wall_ref.at[f, core], ws.at[1], wr.at[1], left),
    ]
    wide[0].start()
    wide[1].start()

    def landed(side):
        return (
            wall_ref.at[from_left, side],
            wall_ref.at[from_right, side],
            wall_ref.at[opposite, side, first],
            wall_ref.at[opposite, side, second],
        )

    for copy in spread:
        copy.wait_recv()
    tab[:VOX, :] = feat_ref[...]
    for n, (a, c) in enumerate(SIDES):
        outer, inner = s + a - 1, f + c - 1
        ok = (outer >= 0) & (outer < NS) & (inner >= 0) & (inner < NF)
        rows_n = beside_ref[n]
        tab[VOX + n * HC : VOX + (n + 1) * HC, :] = jnp.where(ok, rows_n, jnp.zeros_like(rows_n))
    tab_t[...] = tab[...].T
    cot = cot_ref[...]
    rows = lax.broadcasted_iota(jnp.int32, (TAB, VOX), 0)
    scale = 1.0 / math.sqrt(NS * NF * VOX)

    def hot_of(k):
        return (rows == map_ref[k]).astype(jnp.bfloat16)

    def weight_half(side):
        def step(i, _):
            for u in range(2):
                k = side * (KP // 2) + 2 * i + u
                picked = jnp.dot(tab_t[...], hot_of(k), preferred_element_type=jnp.float32).astype(jnp.bfloat16)
                seen[k] = picked
                gw = jnp.dot(picked, cot, preferred_element_type=jnp.float32) * scale
                for q in range(NF):
                    gw_ref[q, pl.ds(pl.multiple_of(k * IL, IL), IL), :] = gw[q * IL : (q + 1) * IL]
            return 0

        lax.fori_loop(0, KP // 4, step, 0)

    weight_half(other)
    order = (2, 1, 3, 0)
    pairs = {}
    for d in order:
        src = gw_ref.at[lax.rem(f + d, NF), pl.ds(other * HALF, HALF), :]
        pairs[d] = remote(src, pbuf.at[d], ps.at[d], pr.at[d], partner)
        pairs[d].start()
    weight_half(core)
    passed = []
    for m, got in enumerate(landed(core)):
        remote(got, got, ws.at[m], wr.at[m], partner).wait_recv()
        if m == 0:
            piece = wall_ref.at[from_left, core, first]
            wide.append(remote(piece, piece, ws.at[2], wr.at[2], right))
            wide[-1].start()
        if m == 1:
            piece = wall_ref.at[from_right, core, second]
            wide.append(remote(piece, piece, ws.at[3], wr.at[3], left))
            wide[-1].start()
        passed.append(remote(got, got, hands.at[m], handr.at[m], partner))
        passed[-1].start()
    half_a, half_b = pl.ds(0, LINE), pl.ds(LINE, LINE)
    across = {}

    def send_x(m, src, dst, target):
        across[m] = remote(src, dst, xs.at[m], xr.at[m], target)
        across[m].start()

    for d in order:
        j = lax.rem(f + d, NF)
        pairs[d].wait_recv()

        def add_pair(i, _):
            here = pl.ds(pl.multiple_of(i * PART, 8), PART)
            mine = pl.ds(pl.multiple_of(core * HALF + i * PART, 8), PART)
            acc0[d, here, :] = gw_ref[j, mine, :] + pbuf[d, here, :]
            return 0

        lax.fori_loop(0, HALF // PART, add_pair, 0)
        if d == 2:
            send_x(0, acc0.at[2, half_a], rbuf.at[0], right)
            send_x(1, acc0.at[2, half_b], rbuf.at[1], left)
        if d == 1:
            send_x(2, acc0.at[1, half_b], xbuf.at[0, half_b], right)
        if d == 3:
            send_x(3, acc0.at[3, half_a], xbuf.at[1, half_a], left)

    for m, d, begin, half, target in ((0, 1, 0, half_a, right), (1, 3, LINE, half_b, left)):
        across[m].wait_recv()

        def add_relay(i, _):
            here = pl.ds(pl.multiple_of(begin + i * PART, 8), PART)
            acc0[d, here, :] += rbuf[m, pl.ds(pl.multiple_of(i * PART, 8), PART), :]
            return 0

        lax.fori_loop(0, LINE // PART, add_relay, 0)
        send_x(4 + m, acc0.at[d, half], xbuf.at[m, half], target)

    for m, there in enumerate(landed(other)):
        remote(there, there, hands.at[m], handr.at[m], partner).wait_recv()
    own[0].wait()
    own[1].wait()
    tg[...] = jnp.zeros_like(tg)

    def spread_group(g, acc):
        hot, high, low = [], [], []
        for u in range(3):
            k = g * 3 + u
            side = k // (SKIP + 1)
            kernel = wall_ref[:, side, k - side * SKIP].reshape(CI, CO)
            acc = acc + lax.dot_general(seen[k], kernel, (((0,), (0,)), ((), ())), preferred_element_type=jnp.float32)
            term = lax.dot_general(cot, kernel, (((1,), (1,)), ((), ())), preferred_element_type=jnp.float32)
            top = term.astype(jnp.bfloat16)
            high.append(top)
            low.append((term - top.astype(jnp.float32)).astype(jnp.bfloat16))
            hot.append(hot_of(k))
        both = jnp.concatenate([jnp.concatenate(high, 0), jnp.concatenate(low, 0)], 1)
        tg[...] += jnp.dot(jnp.concatenate(hot, 1), both, preferred_element_type=jnp.float32)
        return acc

    acc = lax.fori_loop(0, KV // 3, spread_group, jnp.zeros((VOX, CO), jnp.float32))
    conv_ref[...] = acc.astype(jnp.bfloat16)
    own_ref[...] = tg[:VOX, :CI] + tg[:VOX, CI:]
    halo_ref[...] = (tg[VOX:, :CI] + tg[VOX:, CI:]).reshape(8, HC, CI)
    copies = []
    for n, (a, c) in enumerate(SIDES):
        copies.append(remote(halo_ref.at[n], back_ref.at[n], hs.at[n], hr.at[n], shifted(s, f, a - 1, c - 1)))
        copies[-1].start()
    u_copies = []
    for t, needs in enumerate(((3, 4), (2, 5))):
        for m in needs:
            across[m].wait_recv()

        def add_x(i, _):
            here = pl.ds(pl.multiple_of(t * LINE + i * CHUNK, 8), CHUNK)
            acc1[t, i] = acc0[0, here, :] + (xbuf[0, here, :] + xbuf[1, here, :])
            return 0

        lax.fori_loop(0, NY, add_x, 0)
        at, peer = lines[t]
        for d in range(1, NY):
            u_copies.append(remote(acc1.at[t, lax.rem(at + d, NY)], ubuf.at[t, d], us.at[t, d], ur.at[t, d], peer(d)))
            u_copies[-1].start()
    v_copies = []
    for t in range(2):
        for copy in u_copies[t * 7 : t * 7 + 7]:
            copy.wait_recv()
        running = acc1[t, lines[t][0]]
        for d in range(1, NY):
            running = running + ubuf[t, d]
        acc2[t] = running
        at, peer = lines[1 - t]
        vbuf[t, at] = running
        for d in range(1, NZ):
            v_copies.append(remote(acc2.at[t], vbuf.at[t, at], vs.at[t, d], vr.at[t, d], peer(d)))
            v_copies[-1].start()
    g_copies, handed = [], []
    for t in range(2):
        across_at = lines[1 - t][0]
        for d in range(1, NZ):
            got = vbuf.at[t, lax.rem(across_at - d + NZ, NZ)]
            remote(got, got, vs.at[t, d], vr.at[t, d], partner).wait_recv()
        done = vbuf[t, 0]
        for q in range(1, NZ):
            done = done + vbuf[t, q]
        at, peer = lines[t]
        total_ref[core, t, at] = done
        mine = total_ref.at[core, t, at]
        for d in range(1, NY):
            g_copies.append(remote(mine, mine, gs.at[t, d], gr.at[t, d], peer(d)))
            g_copies[-1].start()
        handed.append(remote(mine, mine, cs.at[t, 0], cr.at[t, 0], partner))
        handed[-1].start()
    for copy in copies:
        copy.wait()
    for d in range(1, NY):
        for t in range(2):
            got = total_ref.at[core, t, lax.rem(lines[t][0] - d + NY, NY)]
            remote(got, got, gs.at[t, d], gr.at[t, d], partner).wait_recv()
            handed.append(remote(got, got, cs.at[t, d], cr.at[t, d], partner))
            handed[-1].start()
    for d in range(NY):
        for t in range(2):
            there = total_ref.at[other, t, lax.rem(lines[t][0] - d + NY, NY)]
            remote(there, there, cs.at[t, d], cr.at[t, d], partner).wait_recv()
    for copy in handed + u_copies + v_copies + g_copies:
        copy.wait_send()
    for d in order:
        pairs[d].wait_send()
    for m in range(6):
        across[m].wait_send()
    for copy in passed + wide + spread:
        copy.wait_send()


def dma(*shape):
    return pltpu.SemaphoreType.DMA(shape)


def body(features, cotangent, weight, neighbour_map, send_rows):
    f32, bf16 = jnp.float32, jnp.bfloat16
    pick = (send_rows[:, None] == jnp.arange(VOX)[None, :]).astype(bf16)
    boundary = jnp.dot(pick, features, preferred_element_type=f32).astype(bf16)
    by_offset = jnp.transpose(weight, (1, 0, 2))
    spots = jnp.where(neighbour_map >= VOX + 5 * HC, neighbour_map - HC, neighbour_map)
    spots = jnp.pad(spots, ((0, 1), (0, 0)), constant_values=TAB).reshape(KP, 1, VOX)
    conv_out, own, total, back = pl.pallas_call(
        whole_kernel,
        out_shape=(
            jax.ShapeDtypeStruct((VOX, CO), bf16),
            jax.ShapeDtypeStruct((VOX, CI), f32),
            jax.ShapeDtypeStruct((2, 2, NY, CHUNK, CO), f32),
            jax.ShapeDtypeStruct((8, HC, CI), f32),
        ),
        in_specs=[VMEM] * 5,
        out_specs=(VMEM,) * 4,
        scratch_shapes=[
            pltpu.VMEM((8, HC, CI), bf16),
            pltpu.VMEM((NF, 2, KP // 2, IL, CO), bf16),
            pltpu.VMEM((TAB, CI), bf16),
            pltpu.VMEM((CI, TAB), bf16),
            pltpu.VMEM((KP, CI, VOX), bf16),
            pltpu.VMEM((NF, ROWS, CO), f32),
            pltpu.VMEM((TAB, 2 * CI), f32),
            pltpu.VMEM((8, HC, CI), f32),
            pltpu.VMEM((NF, HALF, CO), f32),
            pltpu.VMEM((NF, HALF, CO), f32),
            pltpu.VMEM((2, LINE, CO), f32),
            pltpu.VMEM((2, HALF, CO), f32),
            pltpu.VMEM((2, NY, CHUNK, CO), f32),
            pltpu.VMEM((2, NY, CHUNK, CO), f32),
            pltpu.VMEM((2, CHUNK, CO), f32),
            pltpu.VMEM((2, NZ, CHUNK, CO), f32),
            dma(8), dma(8), dma(4), dma(4), dma(4), dma(4), dma(2),
        ]
        + [dma(8)] * 2 + [dma(NF)] * 2 + [dma(6)] * 2 + [dma(2, NY)] * 8,
        compiler_params=pltpu.CompilerParams(collective_id=0, has_side_effects=True, vmem_limit_bytes=48 << 20),
        name="whole",
    )(boundary, by_offset, features, spots, cotangent)
    s, f = lax.axis_index("space"), lax.axis_index("fsdp")

    def inside(sign):
        ok = [
            (s + sign * (a - 1) >= 0) & (s + sign * (a - 1) < NS) & (f + sign * (c - 1) >= 0) & (f + sign * (c - 1) < NF)
            for a, c in SIDES
        ]
        return jnp.stack(ok)[:, None, None]

    incoming = jnp.sum(jnp.where(inside(-1), back, 0.0), 0)
    put = (jnp.arange(VOX)[:, None] == send_rows[None, :]).astype(f32)
    settled = own + jnp.dot(put, incoming, preferred_element_type=f32, precision=lax.Precision.HIGHEST)
    grad_weight = jnp.transpose(total.reshape(KP, IL, CO)[:KV], (1, 0, 2))
    return (conv_out, settled.astype(bf16), grad_weight)


def solution(mesh):
    rows = P(("space", "fsdp"), None)
    placed = (rows, rows, P("fsdp", None, None), P(None, ("space", "fsdp")), P(("space", "fsdp")))
    return jax.shard_map(
        body, mesh=mesh, in_specs=placed, out_specs=(rows, rows, P("fsdp", None, None)), check_vma=False
    )
```

```python
import math

import jax
import jax.numpy as jnp
from jax import lax
from jax.experimental import pallas as pl
from jax.experimental.pallas import tpu as pltpu
from jax.sharding import PartitionSpec as P

MESH = pl.DeviceIdType.MESH
VMEM = pl.BlockSpec(memory_space=pltpu.VMEM)
SIDES = [(a, c) for a in range(3) for c in range(3) if (a, c) != (1, 1)]
NS, NF, NY, NZ = 128, 4, 8, 8
VOX, HC, CI, CO, KV, KP = 128, 32, 256, 128, 27, 28
IL = CI // NF
ROWS = KP * IL
HALF = ROWS // 2
LINE = HALF // 2
SKIP = KV // 2
BIG, SMALL = 32, 24
SEGMENTS = ((0, 0, BIG), (1, LINE, BIG), (0, NY * BIG, SMALL), (1, LINE + NY * BIG, SMALL))
FAR_FIRST = (4, 3, 5, 2, 6, 1, 7)
PART = 112
TAB = VOX + 8 * HC


def position():
    s, f = lax.axis_index("space"), lax.axis_index("fsdp")
    core = lax.rem(s, 2)
    y = lax.rem(s // 2, NY)
    z = s // (2 * NY)
    return s, f, core, y, z


def shifted(s, f, ds, df):
    return (lax.rem(s + ds + NS, NS), lax.rem(f + df + NF, NF))


def meet(targets):
    barrier = pltpu.get_barrier_semaphore()
    for target in targets:
        pl.semaphore_signal(barrier, inc=1, device_id=target, device_id_type=MESH)
    pl.semaphore_wait(barrier, len(targets))


def remote(src, dst, send, recv, target):
    return pltpu.make_async_remote_copy(
        src_ref=src, dst_ref=dst, send_sem=send, recv_sem=recv, device_id=target, device_id_type=MESH
    )


def whole_kernel(b_ref, w_ref, feat_ref, map_ref, cot_ref, conv_ref, own_ref, total_ref, back_ref,
                 beside_ref, wall_ref, tab, tab_t, seen, gw_ref, tg, halo_ref, pbuf, acc0, rbuf, xbuf, acc1, ubuf, acc2, vbuf,
                 bs, br, ws, wr, hands, handr, own_sem,
                 hs, hr, ps, pr, xs, xr, us, ur, vs, vr, gs, gr, cs, cr):
    s, f, core, y, z = position()
    other = 1 - core
    partner = (s + 1 - 2 * core, f)
    left, right = shifted(s, f, 0, -1), shifted(s, f, 0, 1)
    from_left, from_right, opposite = left[1], right[1], lax.rem(f + 2, NF)

    def y_peer(d):
        return ((z * NY + lax.rem(y + d, NY)) * 2 + core, f)

    def z_peer(d):
        return ((lax.rem(z + d, NZ) * NY + y) * 2 + core, f)

    lines = ((y, y_peer), (z, z_peer))
    meet(
        [shifted(s, f, a - 1, c - 1) for a, c in SIDES]
        + [partner]
        + [y_peer(d) for d in range(1, NY)]
        + [z_peer(d) for d in range(1, NZ)]
    )
    spread = []
    for n, (a, c) in enumerate(SIDES):
        spread.append(remote(b_ref, beside_ref.at[n], bs.at[n], br.at[n], shifted(s, f, 1 - a, 1 - c)))
        spread[-1].start()
    own = [pltpu.make_async_copy(w_ref.at[pl.ds(h * SKIP, SKIP + 1)], wall_ref.at[f, h], own_sem.at[h]) for h in range(2)]
    own[0].start()
    own[1].start()
    quarter = KP // 4
    first, second = pl.ds(0, quarter), pl.ds(quarter, quarter)
    half_w = w_ref.at[pl.ds(core * SKIP, SKIP + 1)]
    wide = [
        remote(half_w, wall_ref.at[f, core], ws.at[0], wr.at[0], right),
        remote(half_w, wall_ref.at[f, core], ws.at[1], wr.at[1], left),
    ]
    wide[0].start()
    wide[1].start()

    def landed(side):
        return (
            wall_ref.at[from_left, side],
            wall_ref.at[from_right, side],
            wall_ref.at[opposite, side, first],
            wall_ref.at[opposite, side, second],
        )

    for copy in spread:
        copy.wait_recv()
    tab[:VOX, :] = feat_ref[...]
    for n, (a, c) in enumerate(SIDES):
        outer, inner = s + a - 1, f + c - 1
        ok = (outer >= 0) & (outer < NS) & (inner >= 0) & (inner < NF)
        rows_n = beside_ref[n]
        tab[VOX + n * HC : VOX + (n + 1) * HC, :] = jnp.where(ok, rows_n, jnp.zeros_like(rows_n))
    tab_t[...] = tab[...].T
    cot = cot_ref[...]
    rows = lax.broadcasted_iota(jnp.int32, (TAB, VOX), 0)
    scale = 1.0 / math.sqrt(NS * NF * VOX)

    def hot_of(k):
        return (rows == map_ref[k]).astype(jnp.bfloat16)

    def weight_half(side):
        def step(i, _):
            for u in range(2):
                k = side * (KP // 2) + 2 * i + u
                picked = jnp.dot(tab_t[...], hot_of(k), preferred_element_type=jnp.float32).astype(jnp.bfloat16)
                seen[k] = picked
                gw = jnp.dot(picked, cot, preferred_element_type=jnp.float32) * scale
                for q in range(NF):
                    gw_ref[q, pl.ds(pl.multiple_of(k * IL, IL), IL), :] = gw[q * IL : (q + 1) * IL]
            return 0

        lax.fori_loop(0, KP // 4, step, 0)

    weight_half(other)
    order = (2, 1, 3, 0)
    pairs = {}
    for d in order:
        src = gw_ref.at[lax.rem(f + d, NF), pl.ds(other * HALF, HALF), :]
        pairs[d] = remote(src, pbuf.at[d], ps.at[d], pr.at[d], partner)
        pairs[d].start()
    weight_half(core)
    passed = []
    for m, got in enumerate(landed(core)):
        remote(got, got, ws.at[m], wr.at[m], partner).wait_recv()
        if m == 0:
            piece = wall_ref.at[from_left, core, first]
            wide.append(remote(piece, piece, ws.at[2], wr.at[2], right))
            wide[-1].start()
        if m == 1:
            piece = wall_ref.at[from_right, core, second]
            wide.append(remote(piece, piece, ws.at[3], wr.at[3], left))
            wide[-1].start()
        passed.append(remote(got, got, hands.at[m], handr.at[m], partner))
        passed[-1].start()
    across = {}

    def rows_of(g):
        return pl.ds(SEGMENTS[g][1], NY * SEGMENTS[g][2])

    def send_x(m, h, src, dst, target):
        across[m, h] = remote(src, dst, xs.at[m, h], xr.at[m, h], target)
        across[m, h].start()

    for d in order:
        j = lax.rem(f + d, NF)
        pairs[d].wait_recv()

        def add_pair(i, _):
            here = pl.ds(pl.multiple_of(i * PART, 8), PART)
            mine = pl.ds(pl.multiple_of(core * HALF + i * PART, 8), PART)
            acc0[d, here, :] = gw_ref[j, mine, :] + pbuf[d, here, :]
            return 0

        lax.fori_loop(0, HALF // PART, add_pair, 0)
        if d == 2:
            for h in range(2):
                send_x(0, h, acc0.at[2, rows_of(2 * h)], rbuf.at[rows_of(2 * h)], right)
                send_x(1, h, acc0.at[2, rows_of(2 * h + 1)], rbuf.at[rows_of(2 * h + 1)], left)
        if d == 1:
            send_x(2, 0, acc0.at[1, rows_of(1)], xbuf.at[0, rows_of(1)], right)
        if d == 3:
            send_x(3, 0, acc0.at[3, rows_of(0)], xbuf.at[1, rows_of(0)], left)

    for h in range(2):
        if h == 1:
            send_x(2, 1, acc0.at[1, rows_of(3)], xbuf.at[0, rows_of(3)], right)
            send_x(3, 1, acc0.at[3, rows_of(2)], xbuf.at[1, rows_of(2)], left)
        for m, d, target in ((0, 1, right), (1, 3, left)):
            across[m, h].wait_recv()
            t, begin, size = SEGMENTS[2 * h + m]

            def add_relay(i, _):
                here = pl.ds(pl.multiple_of(begin + i * 2 * size, 8), 2 * size)
                acc0[d, here, :] += rbuf[here, :]
                return 0

            lax.fori_loop(0, NY // 2, add_relay, 0)
            send_x(4 + m, h, acc0.at[d, rows_of(2 * h + m)], xbuf.at[m, rows_of(2 * h + m)], target)

    def part(ref, g, p):
        t, begin, size = SEGMENTS[g]
        return ref.at[g, p, pl.ds(0, size)]

    u_copies, v_copies, g_copies, handed = {}, [], [], []

    def enter(g):
        t, begin, size = SEGMENTS[g]
        for m in ((3, 4), (2, 5))[t]:
            across[m, g // 2].wait_recv()

        def add_x(i, _):
            here = pl.ds(pl.multiple_of(begin + i * size, 8), size)
            acc1[g, i, :size] = acc0[0, here, :] + (xbuf[0, here, :] + xbuf[1, here, :])
            return 0

        lax.fori_loop(0, NY, add_x, 0)
        at, peer = lines[t]
        for d in FAR_FIRST:
            u_copies[g, d] = remote(
                part(acc1, g, lax.rem(at + d, NY)), part(ubuf, g, d), us.at[g, d], ur.at[g, d], peer(d)
            )
            u_copies[g, d].start()

    enter(0)
    enter(1)
    for m, there in enumerate(landed(other)):
        remote(there, there, hands.at[m], handr.at[m], partner).wait_recv()
    own[0].wait()
    own[1].wait()
    tg[...] = jnp.zeros_like(tg)

    def spread_group(g, acc):
        hot, high, low = [], [], []
        for u in range(3):
            k = g * 3 + u
            side = k // (SKIP + 1)
            kernel = wall_ref[:, side, k - side * SKIP].reshape(CI, CO)
            acc = acc + lax.dot_general(seen[k], kernel, (((0,), (0,)), ((), ())), preferred_element_type=jnp.float32)
            term = lax.dot_general(cot, kernel, (((1,), (1,)), ((), ())), preferred_element_type=jnp.float32)
            top = term.astype(jnp.bfloat16)
            high.append(top)
            low.append((term - top.astype(jnp.float32)).astype(jnp.bfloat16))
            hot.append(hot_of(k))
        both = jnp.concatenate([jnp.concatenate(high, 0), jnp.concatenate(low, 0)], 1)
        tg[...] += jnp.dot(jnp.concatenate(hot, 1), both, preferred_element_type=jnp.float32)
        return acc

    acc = lax.fori_loop(0, KV // 3, spread_group, jnp.zeros((VOX, CO), jnp.float32))
    conv_ref[...] = acc.astype(jnp.bfloat16)
    own_ref[...] = tg[:VOX, :CI] + tg[:VOX, CI:]
    halo_ref[...] = (tg[VOX:, :CI] + tg[VOX:, CI:]).reshape(8, HC, CI)
    copies = []
    for n, (a, c) in enumerate(SIDES):
        copies.append(remote(halo_ref.at[n], back_ref.at[n], hs.at[n], hr.at[n], shifted(s, f, a - 1, c - 1)))
        copies[-1].start()
    enter(2)
    enter(3)
    for g, (t, begin, size) in enumerate(SEGMENTS):
        running = acc1[g, lines[t][0], :size]
        for d in range(1, NY):
            u_copies[g, d].wait_recv()
            running = running + ubuf[g, d, :size]
        acc2[g, :size] = running
        at, peer = lines[1 - t]
        vbuf[g, at, :size] = running
        for d in FAR_FIRST:
            v_copies.append(
                remote(acc2.at[g, pl.ds(0, size)], part(vbuf, g, at), vs.at[g, d], vr.at[g, d], peer(d))
            )
            v_copies[-1].start()

    def spot(side, g, p):
        t, begin, size = SEGMENTS[g]
        return pl.ds(pl.multiple_of(side * HALF + begin + p * size, 8), size)

    for g, (t, begin, size) in enumerate(SEGMENTS):
        across_at = lines[1 - t][0]
        for d in range(1, NZ):
            got = part(vbuf, g, lax.rem(across_at - d + NZ, NZ))
            remote(got, got, vs.at[g, d], vr.at[g, d], partner).wait_recv()
        done = vbuf[g, 0, :size]
        for q in range(1, NZ):
            done = done + vbuf[g, q, :size]
        at, peer = lines[t]
        total_ref[spot(core, g, at), :] = done
        mine = total_ref.at[spot(core, g, at)]
        for d in FAR_FIRST:
            g_copies.append(remote(mine, mine, gs.at[g, d], gr.at[g, d], peer(d)))
            g_copies[-1].start()
        handed.append(remote(mine, mine, cs.at[g, 0], cr.at[g, 0], partner))
        handed[-1].start()
    for copy in copies:
        copy.wait()
    for g, (t, begin, size) in enumerate(SEGMENTS):
        for d in (1, 7, 2, 6, 3, 5, 4):
            got = total_ref.at[spot(core, g, lax.rem(lines[t][0] - d + NY, NY))]
            remote(got, got, gs.at[g, d], gr.at[g, d], partner).wait_recv()
            handed.append(remote(got, got, cs.at[g, d], cr.at[g, d], partner))
            handed[-1].start()
    for g, (t, begin, size) in enumerate(SEGMENTS):
        for d in range(NY):
            there = total_ref.at[spot(other, g, lax.rem(lines[t][0] - d + NY, NY))]
            remote(there, there, cs.at[g, d], cr.at[g, d], partner).wait_recv()
    for copy in handed + list(u_copies.values()) + v_copies + g_copies:
        copy.wait_send()
    for d in order:
        pairs[d].wait_send()
    for copy in across.values():
        copy.wait_send()
    for copy in passed + wide + spread:
        copy.wait_send()


def dma(*shape):
    return pltpu.SemaphoreType.DMA(shape)


def body(features, cotangent, weight, neighbour_map, send_rows):
    f32, bf16 = jnp.float32, jnp.bfloat16
    pick = (send_rows[:, None] == jnp.arange(VOX)[None, :]).astype(bf16)
    boundary = jnp.dot(pick, features, preferred_element_type=f32).astype(bf16)
    by_offset = jnp.transpose(weight, (1, 0, 2))
    spots = jnp.where(neighbour_map >= VOX + 5 * HC, neighbour_map - HC, neighbour_map)
    spots = jnp.pad(spots, ((0, 1), (0, 0)), constant_values=TAB).reshape(KP, 1, VOX)
    conv_out, own, total, back = pl.pallas_call(
        whole_kernel,
        out_shape=(
            jax.ShapeDtypeStruct((VOX, CO), bf16),
            jax.ShapeDtypeStruct((VOX, CI), f32),
            jax.ShapeDtypeStruct((ROWS, CO), f32),
            jax.ShapeDtypeStruct((8, HC, CI), f32),
        ),
        in_specs=[VMEM] * 5,
        out_specs=(VMEM,) * 4,
        scratch_shapes=[
            pltpu.VMEM((8, HC, CI), bf16),
            pltpu.VMEM((NF, 2, KP // 2, IL, CO), bf16),
            pltpu.VMEM((TAB, CI), bf16),
            pltpu.VMEM((CI, TAB), bf16),
            pltpu.VMEM((KP, CI, VOX), bf16),
            pltpu.VMEM((NF, ROWS, CO), f32),
            pltpu.VMEM((TAB, 2 * CI), f32),
            pltpu.VMEM((8, HC, CI), f32),
            pltpu.VMEM((NF, HALF, CO), f32),
            pltpu.VMEM((NF, HALF, CO), f32),
            pltpu.VMEM((HALF, CO), f32),
            pltpu.VMEM((2, HALF, CO), f32),
            pltpu.VMEM((4, NY, BIG, CO), f32),
            pltpu.VMEM((4, NY, BIG, CO), f32),
            pltpu.VMEM((4, BIG, CO), f32),
            pltpu.VMEM((4, NZ, BIG, CO), f32),
            dma(8), dma(8), dma(4), dma(4), dma(4), dma(4), dma(2),
        ]
        + [dma(8)] * 2 + [dma(NF)] * 2 + [dma(6, 2)] * 2 + [dma(4, NY)] * 8,
        compiler_params=pltpu.CompilerParams(collective_id=0, has_side_effects=True, vmem_limit_bytes=48 << 20),
        name="whole",
    )(boundary, by_offset, features, spots, cotangent)
    s, f = lax.axis_index("space"), lax.axis_index("fsdp")

    def inside(sign):
        ok = [
            (s + sign * (a - 1) >= 0) & (s + sign * (a - 1) < NS) & (f + sign * (c - 1) >= 0) & (f + sign * (c - 1) < NF)
            for a, c in SIDES
        ]
        return jnp.stack(ok)[:, None, None]

    incoming = jnp.sum(jnp.where(inside(-1), back, 0.0), 0)
    put = (jnp.arange(VOX)[:, None] == send_rows[None, :]).astype(f32)
    settled = own + jnp.dot(put, incoming, preferred_element_type=f32, precision=lax.Precision.HIGHEST)
    grad_weight = jnp.transpose(total.reshape(KP, IL, CO)[:KV], (1, 0, 2))
    return (conv_out, settled.astype(bf16), grad_weight)


def solution(mesh):
    rows = P(("space", "fsdp"), None)
    placed = (rows, rows, P("fsdp", None, None), P(None, ("space", "fsdp")), P(("space", "fsdp")))
    return jax.shard_map(
        body, mesh=mesh, in_specs=placed, out_specs=(rows, rows, P("fsdp", None, None)), check_vma=False
    )
```

```python
import math

import jax
import jax.numpy as jnp
from jax import lax
from jax.experimental import pallas as pl
from jax.experimental.pallas import tpu as pltpu
from jax.sharding import PartitionSpec as P

MESH = pl.DeviceIdType.MESH
VMEM = pl.BlockSpec(memory_space=pltpu.VMEM)
SIDES = [(a, c) for a in range(3) for c in range(3) if (a, c) != (1, 1)]
NS, NF, NY, NZ = 128, 4, 8, 8
VOX, HC, CI, CO, KV, KP = 128, 32, 256, 128, 27, 28
IL = CI // NF
ROWS = KP * IL
HALF = ROWS // 2
LINE = HALF // 2
SKIP = KV // 2
BATCH = 7
BIG, SMALL = 32, 24
SEGMENTS = ((0, 0, BIG), (1, LINE, BIG), (0, NY * BIG, SMALL), (1, LINE + NY * BIG, SMALL))
FAR_FIRST = (4, 3, 5, 2, 6, 1, 7)
PART = 112
TAB = VOX + 8 * HC


def position():
    s, f = lax.axis_index("space"), lax.axis_index("fsdp")
    core = lax.rem(s, 2)
    y = lax.rem(s // 2, NY)
    z = s // (2 * NY)
    return s, f, core, y, z


def shifted(s, f, ds, df):
    return (lax.rem(s + ds + NS, NS), lax.rem(f + df + NF, NF))


def meet(targets):
    barrier = pltpu.get_barrier_semaphore()
    for target in targets:
        pl.semaphore_signal(barrier, inc=1, device_id=target, device_id_type=MESH)
    pl.semaphore_wait(barrier, len(targets))


def remote(src, dst, send, recv, target):
    return pltpu.make_async_remote_copy(
        src_ref=src, dst_ref=dst, send_sem=send, recv_sem=recv, device_id=target, device_id_type=MESH
    )


def whole_kernel(b_ref, w_ref, feat_in, map_in, cot_in, conv_ref, own_ref, total_ref, back_ref,
                 map_ref, cot_ref, in_sem, beside_ref, wall_ref, tab, tab_t, seen, gw_ref, tg, halo_ref, pbuf, acc0, rbuf, xbuf, acc1, ubuf, acc2, vbuf,
                 bs, br, ws, wr, hands, handr, own_sem,
                 hs, hr, ps, pr, xs, xr, us, ur, vs, vr, gs, gr, cs, cr):
    s, f, core, y, z = position()
    other = 1 - core
    partner = (s + 1 - 2 * core, f)
    left, right = shifted(s, f, 0, -1), shifted(s, f, 0, 1)
    from_left, from_right, opposite = left[1], right[1], lax.rem(f + 2, NF)

    def y_peer(d):
        return ((z * NY + lax.rem(y + d, NY)) * 2 + core, f)

    def z_peer(d):
        return ((lax.rem(z + d, NZ) * NY + y) * 2 + core, f)

    lines = ((y, y_peer), (z, z_peer))
    taken = [
        pltpu.make_async_copy(feat_in, tab.at[pl.ds(0, VOX)], in_sem.at[0]),
        pltpu.make_async_copy(map_in, map_ref, in_sem.at[1]),
        pltpu.make_async_copy(cot_in, cot_ref, in_sem.at[2]),
    ]
    for copy in taken:
        copy.start()
    meet(
        [shifted(s, f, a - 1, c - 1) for a, c in SIDES]
        + [partner]
        + [y_peer(d) for d in range(1, NY)]
        + [z_peer(d) for d in range(1, NZ)]
    )
    spread = []
    for n, (a, c) in enumerate(SIDES):
        spread.append(remote(b_ref, beside_ref.at[n], bs.at[n], br.at[n], shifted(s, f, 1 - a, 1 - c)))
        spread[-1].start()
    own = [pltpu.make_async_copy(w_ref.at[pl.ds(h * SKIP, SKIP + 1)], wall_ref.at[f, h], own_sem.at[h]) for h in range(2)]
    own[0].start()
    own[1].start()
    quarter = KP // 4
    first, second = pl.ds(0, quarter), pl.ds(quarter, quarter)
    half_w = w_ref.at[pl.ds(core * SKIP, SKIP + 1)]
    wide = [
        remote(half_w, wall_ref.at[f, core], ws.at[0], wr.at[0], right),
        remote(half_w, wall_ref.at[f, core], ws.at[1], wr.at[1], left),
    ]
    wide[0].start()
    wide[1].start()

    def landed(side):
        return (
            wall_ref.at[from_left, side],
            wall_ref.at[from_right, side],
            wall_ref.at[opposite, side, first],
            wall_ref.at[opposite, side, second],
        )

    for copy in spread:
        copy.wait_recv()
    for copy in taken:
        copy.wait()
    for n, (a, c) in enumerate(SIDES):
        outer, inner = s + a - 1, f + c - 1
        ok = (outer >= 0) & (outer < NS) & (inner >= 0) & (inner < NF)
        rows_n = beside_ref[n]
        tab[VOX + n * HC : VOX + (n + 1) * HC, :] = jnp.where(ok, rows_n, jnp.zeros_like(rows_n))
    tab_t[...] = tab[...].T
    cot = cot_ref[...]
    rows = lax.broadcasted_iota(jnp.int32, (TAB, VOX), 0)
    scale = 1.0 / math.sqrt(NS * NF * VOX)

    def hot_of(k):
        return (rows == map_ref[k]).astype(jnp.bfloat16)

    def weight_half(side):
        def step(i, _):
            first = side * (KP // 2) + i * BATCH
            hot = jnp.concatenate([hot_of(first + u) for u in range(BATCH)], 1)
            picked = jnp.dot(tab_t[...], hot, preferred_element_type=jnp.float32).astype(jnp.bfloat16)
            for u in range(BATCH):
                k = first + u
                one = picked[:, u * VOX : (u + 1) * VOX]
                seen[k] = one
                gw = jnp.dot(one, cot, preferred_element_type=jnp.float32) * scale
                for q in range(NF):
                    gw_ref[q, pl.ds(pl.multiple_of(k * IL, IL), IL), :] = gw[q * IL : (q + 1) * IL]
            return 0

        lax.fori_loop(0, KP // 2 // BATCH, step, 0)

    weight_half(other)
    order = (2, 1, 3, 0)
    pairs = {}
    for d in order:
        src = gw_ref.at[lax.rem(f + d, NF), pl.ds(other * HALF, HALF), :]
        pairs[d] = remote(src, pbuf.at[d], ps.at[d], pr.at[d], partner)
        pairs[d].start()
    weight_half(core)
    passed = []
    for m, got in enumerate(landed(core)):
        remote(got, got, ws.at[m], wr.at[m], partner).wait_recv()
        if m == 0:
            piece = wall_ref.at[from_left, core, first]
            wide.append(remote(piece, piece, ws.at[2], wr.at[2], right))
            wide[-1].start()
        if m == 1:
            piece = wall_ref.at[from_right, core, second]
            wide.append(remote(piece, piece, ws.at[3], wr.at[3], left))
            wide[-1].start()
        passed.append(remote(got, got, hands.at[m], handr.at[m], partner))
        passed[-1].start()
    across = {}

    def rows_of(g):
        return pl.ds(SEGMENTS[g][1], NY * SEGMENTS[g][2])

    def send_x(m, h, src, dst, target):
        across[m, h] = remote(src, dst, xs.at[m, h], xr.at[m, h], target)
        across[m, h].start()

    for d in order:
        j = lax.rem(f + d, NF)
        pairs[d].wait_recv()

        def add_pair(i, _):
            here = pl.ds(pl.multiple_of(i * PART, 8), PART)
            mine = pl.ds(pl.multiple_of(core * HALF + i * PART, 8), PART)
            acc0[d, here, :] = gw_ref[j, mine, :] + pbuf[d, here, :]
            return 0

        lax.fori_loop(0, HALF // PART, add_pair, 0)
        if d == 2:
            for h in range(2):
                send_x(0, h, acc0.at[2, rows_of(2 * h)], rbuf.at[rows_of(2 * h)], right)
                send_x(1, h, acc0.at[2, rows_of(2 * h + 1)], rbuf.at[rows_of(2 * h + 1)], left)
        if d == 1:
            send_x(2, 0, acc0.at[1, rows_of(1)], xbuf.at[0, rows_of(1)], right)
        if d == 3:
            send_x(3, 0, acc0.at[3, rows_of(0)], xbuf.at[1, rows_of(0)], left)

    for h in range(2):
        if h == 1:
            send_x(2, 1, acc0.at[1, rows_of(3)], xbuf.at[0, rows_of(3)], right)
            send_x(3, 1, acc0.at[3, rows_of(2)], xbuf.at[1, rows_of(2)], left)
        for m, d, target in ((0, 1, right), (1, 3, left)):
            across[m, h].wait_recv()
            t, begin, size = SEGMENTS[2 * h + m]

            def add_relay(i, _):
                here = pl.ds(pl.multiple_of(begin + i * 2 * size, 8), 2 * size)
                acc0[d, here, :] += rbuf[here, :]
                return 0

            lax.fori_loop(0, NY // 2, add_relay, 0)
            send_x(4 + m, h, acc0.at[d, rows_of(2 * h + m)], xbuf.at[m, rows_of(2 * h + m)], target)

    def part(ref, g, p):
        t, begin, size = SEGMENTS[g]
        return ref.at[g, p, pl.ds(0, size)]

    u_copies, v_copies, g_copies, handed = {}, [], [], []

    def enter(g):
        t, begin, size = SEGMENTS[g]
        for m in ((3, 4), (2, 5))[t]:
            across[m, g // 2].wait_recv()

        def add_x(i, _):
            here = pl.ds(pl.multiple_of(begin + i * size, 8), size)
            acc1[g, i, :size] = acc0[0, here, :] + (xbuf[0, here, :] + xbuf[1, here, :])
            return 0

        lax.fori_loop(0, NY, add_x, 0)
        at, peer = lines[t]
        for d in FAR_FIRST:
            u_copies[g, d] = remote(
                part(acc1, g, lax.rem(at + d, NY)), part(ubuf, g, d), us.at[g, d], ur.at[g, d], peer(d)
            )
            u_copies[g, d].start()

    enter(0)
    enter(1)
    for m, there in enumerate(landed(other)):
        remote(there, there, hands.at[m], handr.at[m], partner).wait_recv()
    own[0].wait()
    own[1].wait()
    tg[...] = jnp.zeros_like(tg)

    def spread_group(g, acc):
        hot, high, low = [], [], []
        for u in range(3):
            k = g * 3 + u
            side = k // (SKIP + 1)
            kernel = wall_ref[:, side, k - side * SKIP].reshape(CI, CO)
            acc = acc + lax.dot_general(seen[k], kernel, (((0,), (0,)), ((), ())), preferred_element_type=jnp.float32)
            term = lax.dot_general(cot, kernel, (((1,), (1,)), ((), ())), preferred_element_type=jnp.float32)
            top = term.astype(jnp.bfloat16)
            high.append(top)
            low.append((term - top.astype(jnp.float32)).astype(jnp.bfloat16))
            hot.append(hot_of(k))
        both = jnp.concatenate([jnp.concatenate(high, 0), jnp.concatenate(low, 0)], 1)
        tg[...] += jnp.dot(jnp.concatenate(hot, 1), both, preferred_element_type=jnp.float32)
        return acc

    acc = lax.fori_loop(0, KV // 3, spread_group, jnp.zeros((VOX, CO), jnp.float32))
    conv_ref[...] = acc.astype(jnp.bfloat16)
    own_ref[...] = tg[:VOX, :CI] + tg[:VOX, CI:]
    halo_ref[...] = (tg[VOX:, :CI] + tg[VOX:, CI:]).reshape(8, HC, CI)
    copies = []
    for n, (a, c) in enumerate(SIDES):
        copies.append(remote(halo_ref.at[n], back_ref.at[n], hs.at[n], hr.at[n], shifted(s, f, a - 1, c - 1)))
        copies[-1].start()
    enter(2)
    enter(3)
    for g, (t, begin, size) in enumerate(SEGMENTS):
        running = acc1[g, lines[t][0], :size]
        for d in range(1, NY):
            u_copies[g, d].wait_recv()
            running = running + ubuf[g, d, :size]
        acc2[g, :size] = running
        at, peer = lines[1 - t]
        vbuf[g, at, :size] = running
        for d in FAR_FIRST:
            v_copies.append(
                remote(acc2.at[g, pl.ds(0, size)], part(vbuf, g, at), vs.at[g, d], vr.at[g, d], peer(d))
            )
            v_copies[-1].start()

    def spot(side, g, p):
        t, begin, size = SEGMENTS[g]
        return pl.ds(pl.multiple_of(side * HALF + begin + p * size, 8), size)

    for g, (t, begin, size) in enumerate(SEGMENTS):
        across_at = lines[1 - t][0]
        for d in range(1, NZ):
            got = part(vbuf, g, lax.rem(across_at - d + NZ, NZ))
            remote(got, got, vs.at[g, d], vr.at[g, d], partner).wait_recv()
        done = vbuf[g, 0, :size]
        for q in range(1, NZ):
            done = done + vbuf[g, q, :size]
        at, peer = lines[t]
        total_ref[spot(core, g, at), :] = done
        mine = total_ref.at[spot(core, g, at)]
        for d in FAR_FIRST:
            g_copies.append(remote(mine, mine, gs.at[g, d], gr.at[g, d], peer(d)))
            g_copies[-1].start()
        handed.append(remote(mine, mine, cs.at[g, 0], cr.at[g, 0], partner))
        handed[-1].start()
    for copy in copies:
        copy.wait()
    for g, (t, begin, size) in enumerate(SEGMENTS):
        for d in (1, 7, 2, 6, 3, 5, 4):
            got = total_ref.at[spot(core, g, lax.rem(lines[t][0] - d + NY, NY))]
            remote(got, got, gs.at[g, d], gr.at[g, d], partner).wait_recv()
            handed.append(remote(got, got, cs.at[g, d], cr.at[g, d], partner))
            handed[-1].start()
    for g, (t, begin, size) in enumerate(SEGMENTS):
        for d in range(NY):
            there = total_ref.at[spot(other, g, lax.rem(lines[t][0] - d + NY, NY))]
            remote(there, there, cs.at[g, d], cr.at[g, d], partner).wait_recv()
    for copy in handed + list(u_copies.values()) + v_copies + g_copies:
        copy.wait_send()
    for d in order:
        pairs[d].wait_send()
    for copy in across.values():
        copy.wait_send()
    for copy in passed + wide + spread:
        copy.wait_send()


def dma(*shape):
    return pltpu.SemaphoreType.DMA(shape)


def body(features, cotangent, weight, neighbour_map, send_rows):
    f32, bf16 = jnp.float32, jnp.bfloat16
    pick = (send_rows[:, None] == jnp.arange(VOX)[None, :]).astype(bf16)
    boundary = jnp.dot(pick, features, preferred_element_type=f32).astype(bf16)
    by_offset = jnp.transpose(weight, (1, 0, 2))
    spots = jnp.where(neighbour_map >= VOX + 5 * HC, neighbour_map - HC, neighbour_map)
    spots = jnp.pad(spots, ((0, 1), (0, 0)), constant_values=TAB).reshape(KP, 1, VOX)
    conv_out, own, total, back = pl.pallas_call(
        whole_kernel,
        out_shape=(
            jax.ShapeDtypeStruct((VOX, CO), bf16),
            jax.ShapeDtypeStruct((VOX, CI), f32),
            jax.ShapeDtypeStruct((ROWS, CO), f32),
            jax.ShapeDtypeStruct((8, HC, CI), f32),
        ),
        in_specs=[VMEM] + [pl.BlockSpec(memory_space=pl.ANY)] * 4,
        out_specs=(VMEM,) * 4,
        scratch_shapes=[
            pltpu.VMEM((KP, 1, VOX), jnp.int32),
            pltpu.VMEM((VOX, CO), bf16),
            dma(3),
            pltpu.VMEM((8, HC, CI), bf16),
            pltpu.VMEM((NF, 2, KP // 2, IL, CO), bf16),
            pltpu.VMEM((TAB, CI), bf16),
            pltpu.VMEM((CI, TAB), bf16),
            pltpu.VMEM((KP, CI, VOX), bf16),
            pltpu.VMEM((NF, ROWS, CO), f32),
            pltpu.VMEM((TAB, 2 * CI), f32),
            pltpu.VMEM((8, HC, CI), f32),
            pltpu.VMEM((NF, HALF, CO), f32),
            pltpu.VMEM((NF, HALF, CO), f32),
            pltpu.VMEM((HALF, CO), f32),
            pltpu.VMEM((2, HALF, CO), f32),
            pltpu.VMEM((4, NY, BIG, CO), f32),
            pltpu.VMEM((4, NY, BIG, CO), f32),
            pltpu.VMEM((4, BIG, CO), f32),
            pltpu.VMEM((4, NZ, BIG, CO), f32),
            dma(8), dma(8), dma(4), dma(4), dma(4), dma(4), dma(2),
        ]
        + [dma(8)] * 2 + [dma(NF)] * 2 + [dma(6, 2)] * 2 + [dma(4, NY)] * 8,
        compiler_params=pltpu.CompilerParams(collective_id=0, has_side_effects=True, vmem_limit_bytes=48 << 20),
        name="whole",
    )(boundary, by_offset, features, spots, cotangent)
    s, f = lax.axis_index("space"), lax.axis_index("fsdp")

    def inside(sign):
        ok = [
            (s + sign * (a - 1) >= 0) & (s + sign * (a - 1) < NS) & (f + sign * (c - 1) >= 0) & (f + sign * (c - 1) < NF)
            for a, c in SIDES
        ]
        return jnp.stack(ok)[:, None, None]

    incoming = jnp.sum(jnp.where(inside(-1), back, 0.0), 0)
    put = (jnp.arange(VOX)[:, None] == send_rows[None, :]).astype(f32)
    settled = own + jnp.dot(put, incoming, preferred_element_type=f32, precision=lax.Precision.HIGHEST)
    grad_weight = jnp.transpose(total.reshape(KP, IL, CO)[:KV], (1, 0, 2))
    return (conv_out, settled.astype(bf16), grad_weight)


def solution(mesh):
    rows = P(("space", "fsdp"), None)
    placed = (rows, rows, P("fsdp", None, None), P(None, ("space", "fsdp")), P(("space", "fsdp")))
    return jax.shard_map(
        body, mesh=mesh, in_specs=placed, out_specs=(rows, rows, P("fsdp", None, None)), check_vma=False
    )
```
